32 devices in a mesh: dp: 8 (over z, core), tensor: 4 (over y, x).
Axes of the slice: x: 2, y: 2, z: 4, core: 2. Of those that a mesh axis runs over, the one named last changes fastest.
Arguments:
- hidden_in: bfloat16 [32, 1024, 2048], P('dp', 'tensor'), may hold values from -6 to 6
- cotangent: bfloat16 [32, 1024, 2048], P('dp', 'tensor'), may hold values from -6 to 6
- lengths: int32 [32], P('dp'), may hold values from 256 to 1024, as said below
- adapter_ids: int32 [32], P('dp'), may hold values from 0 to 7
- attn_norm: bfloat16 [2048], replicated, may hold values from 0.5 to 1.5
- q_norm: bfloat16 [128], replicated, may hold values from 0.5 to 1.5
- k_norm: bfloat16 [128], replicated, may hold values from 0.5 to 1.5
- ffn_norm: bfloat16 [2048], replicated, may hold values from 0.5 to 1.5
- w_q: bfloat16 [2048, 2048], P(None, 'tensor'), may hold values from -0.125 to 0.125
- key_weight: bfloat16 [2048, 1024], P(None, 'tensor'), may hold values from -0.125 to 0.125
- value_weight: bfloat16 [2048, 1024], P(None, 'tensor'), may hold values from -0.125 to 0.125
- w_o: bfloat16 [2048, 2048], P('tensor'), may hold values from -0.5 to 0.5
- w_gate: bfloat16 [6144, 2048], P('tensor'), may hold values from -0.125 to 0.125
- w_up: bfloat16 [6144, 2048], P('tensor'), may hold values from -0.125 to 0.125
- w_down: bfloat16 [6144, 2048], P('tensor'), may hold values from -0.15625 to 0.15625
- a_q: bfloat16 [8, 2048, 16], replicated, may hold values from -0.125 to 0.125
- b_q: bfloat16 [8, 16, 2048], P(None, None, 'tensor'), may hold values from -0.75 to 0.75
- a_k: bfloat16 [8, 2048, 16], replicated, may hold values from -0.125 to 0.125
- key_second_factor: bfloat16 [8, 16, 1024], P(None, None, 'tensor'), may hold values from -0.75 to 0.75
- a_v: bfloat16 [8, 2048, 16], replicated, may hold values from -0.125 to 0.125
- value_second_factor: bfloat16 [8, 16, 1024], P(None, None, 'tensor'), may hold values from -0.75 to 0.75
- a_o: bfloat16 [8, 2048, 16], P(None, 'tensor'), may hold values from -0.5 to 0.5
- b_o: bfloat16 [8, 16, 2048], replicated, may hold values from -0.75 to 0.75
- a_gate: bfloat16 [8, 2048, 16], replicated, may hold values from -0.125 to 0.125
- b_gate: bfloat16 [6144, 8, 16], P('tensor'), may hold values from -0.75 to 0.75
- a_up: bfloat16 [8, 2048, 16], replicated, may hold values from -0.125 to 0.125
- b_up: bfloat16 [6144, 8, 16], P('tensor'), may hold values from -0.75 to 0.75
- a_down: bfloat16 [6144, 8, 16], P('tensor'), may hold values from -0.15625 to 0.15625
- b_down: bfloat16 [8, 16, 2048], replicated, may hold values from -0.75 to 0.75
Outputs:
- output: bfloat16 [32, 1024, 2048], P('dp', 'tensor')
- d_input: bfloat16 [32, 1024, 2048], P('dp', 'tensor')
- g_a_q: float32 [8, 2048, 16], replicated
- g_b_q: float32 [8, 16, 2048], P(None, None, 'tensor')
- g_a_k: float32 [8, 2048, 16], replicated
- g_b_k: float32 [8, 16, 1024], P(None, None, 'tensor')
- g_a_v: float32 [8, 2048, 16], replicated
- g_b_v: float32 [8, 16, 1024], P(None, None, 'tensor')
- g_a_o: float32 [8, 2048, 16], P(None, 'tensor')
- g_b_o: float32 [8, 16, 2048], replicated
- g_a_gate: float32 [8, 2048, 16], replicated
- g_b_gate: float32 [6144, 8, 16], P('tensor')
- g_a_up: float32 [8, 2048, 16], replicated
- g_b_up: float32 [6144, 8, 16], P('tensor')
- g_a_down: float32 [6144, 8, 16], P('tensor')
- g_b_down: float32 [8, 16, 2048], replicated
The draws below stay inside these ranges and needn't reach their ends.
Inputs may be any that keep to these rules, and one draw needn't show every extreme that they name: `lengths`: every row holds between 256 and 1024 valid tokens; some row holds exactly 1024 and some exactly 256.
All inputs are finite; a program needn't handle non-finite values.
Results may differ from the reference program's by a relative error of at most 0.02.
Values may be sent and summed in bfloat16 or wider, within the bound.
No kernel may reach another device: no remote copies, remote signals or barrier semaphores. Data moves between devices by JAX's collectives and lax.ppermute only.
A program may use at most 384 MiB of HBM per device.

```python
import jax
import jax.numpy as jnp
from jax import lax

MODEL_WIDTH = 2048
HQ = 16
KEY_VALUE_HEADS = 8
HEAD_SIZE = 128
FF = 6144
ADAPTER_RANK = 16
ADAPTER_TOTAL = 8
ROW_SLOTS = 1024
LMIN = 256
ROWS_DEV = 4
ROWS = 32


def draw_lengths(key, part):
    drawn = jax.random.randint(key, (ROWS,), LMIN, ROW_SLOTS + 1).astype(jnp.int32)
    return drawn.at[0].set(ROW_SLOTS).at[1].set(LMIN)


def place_ends(values, rng, smallest, top_value):
    index_at = [jax.random.randint(jax.random.fold_in(rng, axis), (), 0, length) for axis, length in enumerate(values.shape)]
    widest = values.shape.index(max(values.shape))
    next_to = index_at[:widest] + [(index_at[widest] + 1) % values.shape[widest]] + index_at[widest + 1:]
    return values.at[tuple(index_at)].set(smallest).at[tuple(next_to)].set(top_value)


def block_scale(key, extent, cuts, smallest, high):
    level = 1.0
    for axis_at, shards_of in cuts:
        steps = jax.random.uniform(jax.random.fold_in(jax.random.fold_in(key, 6), axis_at), (shards_of,), jnp.float32, smallest / len(cuts), high / len(cuts))
        level = level * jnp.repeat(jnp.exp(steps), extent[axis_at] // shards_of).reshape((-1,) + (1,) * (len(extent) - 1 - axis_at))
    return level


def scatter_about(stream_key, shape, scale, bound, shards=(), held_as=jnp.bfloat16):
    loudness = block_scale(stream_key, shape, shards, -0.22, 0.18) if shards else 1.0
    values = jax.random.normal(stream_key, shape, jnp.float32) * scale * loudness
    return jnp.minimum(jnp.maximum(values, -bound), bound).astype(held_as)


def setup_inputs(seed: int = 0) -> dict:
    arg_keys = jax.random.split(jax.random.key(seed), 30)
    return {
        "hidden_in": scatter_about(arg_keys[0], (ROWS, ROW_SLOTS, MODEL_WIDTH), 1.0, 6.0, ((0, 8), (1, 4))),
        "cotangent": scatter_about(arg_keys[1], (ROWS, ROW_SLOTS, MODEL_WIDTH), 1.0, 6.0, ((0, 8), (1, 4))),
        "lengths": draw_lengths(jax.random.fold_in(arg_keys[29], 71), 0),
        "adapter_ids": place_ends(jax.random.randint(arg_keys[3], (ROWS,), 0, ADAPTER_TOTAL), jax.random.fold_in(arg_keys[3], 1), 0, ADAPTER_TOTAL - 1).astype(jnp.int32),
        "attn_norm": jnp.clip(1.0 + 0.1 * jax.random.normal(arg_keys[4], (MODEL_WIDTH,), jnp.float32), 0.5, 1.5).astype(jnp.bfloat16),
        "q_norm": jnp.clip(1.0 + 0.1 * jax.random.normal(arg_keys[5], (HEAD_SIZE,), jnp.float32), 0.5, 1.5).astype(jnp.bfloat16),
        "k_norm": jnp.clip(1.0 + 0.1 * jax.random.normal(arg_keys[6], (HEAD_SIZE,), jnp.float32), 0.5, 1.5).astype(jnp.bfloat16),
        "ffn_norm": jnp.clip(1.0 + 0.1 * jax.random.normal(arg_keys[7], (MODEL_WIDTH,), jnp.float32), 0.5, 1.5).astype(jnp.bfloat16),
        "w_q": scatter_about(arg_keys[8], (MODEL_WIDTH, HQ * HEAD_SIZE), MODEL_WIDTH ** -0.5, 0.125, ((1, 4),)),
        "key_weight": scatter_about(arg_keys[9], (MODEL_WIDTH, KEY_VALUE_HEADS * HEAD_SIZE), MODEL_WIDTH ** -0.5, 0.125, ((1, 4),)),
        "value_weight": scatter_about(arg_keys[10], (MODEL_WIDTH, KEY_VALUE_HEADS * HEAD_SIZE), MODEL_WIDTH ** -0.5, 0.125, ((1, 4),)),
        "w_o": scatter_about(arg_keys[11], (HQ * HEAD_SIZE, MODEL_WIDTH), (HQ * HEAD_SIZE // 16) ** -0.5, 0.5, ((0, 4),)),
        "w_gate": scatter_about(arg_keys[12], (FF, MODEL_WIDTH), MODEL_WIDTH ** -0.5, 0.125, ((0, 4),)),
        "w_up": scatter_about(arg_keys[13], (FF, MODEL_WIDTH), MODEL_WIDTH ** -0.5, 0.125, ((0, 4),)),
        "w_down": scatter_about(arg_keys[14], (FF, MODEL_WIDTH), (FF // 4) ** -0.5, 0.15625, ((0, 4),)),
        "a_q": scatter_about(arg_keys[15], (ADAPTER_TOTAL, MODEL_WIDTH, ADAPTER_RANK), MODEL_WIDTH ** -0.5, 0.125),
        "b_q": scatter_about(arg_keys[16], (ADAPTER_TOTAL, ADAPTER_RANK, HQ * HEAD_SIZE), (4 * ADAPTER_RANK) ** -0.5, 0.75, ((2, 4),)),
        "a_k": scatter_about(arg_keys[17], (ADAPTER_TOTAL, MODEL_WIDTH, ADAPTER_RANK), MODEL_WIDTH ** -0.5, 0.125),
        "key_second_factor": scatter_about(arg_keys[18], (ADAPTER_TOTAL, ADAPTER_RANK, KEY_VALUE_HEADS * HEAD_SIZE), (4 * ADAPTER_RANK) ** -0.5, 0.75, ((2, 4),)),
        "a_v": scatter_about(arg_keys[19], (ADAPTER_TOTAL, MODEL_WIDTH, ADAPTER_RANK), MODEL_WIDTH ** -0.5, 0.125),
        "value_second_factor": scatter_about(arg_keys[20], (ADAPTER_TOTAL, ADAPTER_RANK, KEY_VALUE_HEADS * HEAD_SIZE), (4 * ADAPTER_RANK) ** -0.5, 0.75, ((2, 4),)),
        "a_o": scatter_about(arg_keys[21], (ADAPTER_TOTAL, HQ * HEAD_SIZE, ADAPTER_RANK), (HQ * HEAD_SIZE // 16) ** -0.5, 0.5, ((1, 4),)),
        "b_o": scatter_about(arg_keys[22], (ADAPTER_TOTAL, ADAPTER_RANK, MODEL_WIDTH), (4 * ADAPTER_RANK) ** -0.5, 0.75),
        "a_gate": scatter_about(arg_keys[23], (ADAPTER_TOTAL, MODEL_WIDTH, ADAPTER_RANK), MODEL_WIDTH ** -0.5, 0.125),
        "b_gate": scatter_about(arg_keys[24], (FF, ADAPTER_TOTAL, ADAPTER_RANK), (4 * ADAPTER_RANK) ** -0.5, 0.75, ((0, 4),)),
        "a_up": scatter_about(arg_keys[25], (ADAPTER_TOTAL, MODEL_WIDTH, ADAPTER_RANK), MODEL_WIDTH ** -0.5, 0.125),
        "b_up": scatter_about(arg_keys[26], (FF, ADAPTER_TOTAL, ADAPTER_RANK), (4 * ADAPTER_RANK) ** -0.5, 0.75, ((0, 4),)),
        "a_down": scatter_about(arg_keys[27], (FF, ADAPTER_TOTAL, ADAPTER_RANK), (FF // 4) ** -0.5, 0.15625, ((0, 4),)),
        "b_down": scatter_about(arg_keys[28], (ADAPTER_TOTAL, ADAPTER_RANK, MODEL_WIDTH), (4 * ADAPTER_RANK) ** -0.5, 0.75),
    }


epsilon = 1e-06
rope_base = 1000000.0
highest = lax.Precision.HIGHEST

@jax.custom_vjp
def low(v):
    return lax.optimization_barrier(v.astype(jnp.bfloat16)).astype(jnp.float32)

@jax.custom_vjp
def low_back(v):
    return v

def low_keep(v):
    return (low(v), None)

def low_pass(kept, grad):
    return (grad,)

def back_keep(v):
    return (v, None)

def back_low(kept, grad):
    return (low(grad),)
low.defvjp(low_keep, low_pass)
low_back.defvjp(back_keep, back_low)

def normed(values, gain):
    return values * lax.rsqrt(lax.optimization_barrier(jnp.mean(values * values, axis=-1, keepdims=True)) + epsilon) * gain

def rope_tables(slot_count, head_dim):
    position = jnp.arange(slot_count).astype(jnp.float32)
    exponent = jnp.arange(head_dim // 2).astype(jnp.float32) * (2.0 / head_dim)
    angles = position[:, None] * (rope_base ** (-exponent))[None, :]
    cosine = jnp.cos(angles)
    sine = jnp.sin(angles)
    return (jnp.concatenate([cosine, cosine], -1), jnp.concatenate([sine, sine], -1))

def rotate(values, cosine, sine):
    half_dim = values.shape[-1] // 2
    turned = jnp.concatenate([-values[..., half_dim:], values[..., :half_dim]], -1)
    return values * cosine[:, None, :] + turned * sine[:, None, :]

def head_prep(raw, gain, cosine, sine):
    head_dim = gain.shape[0]
    shaped = raw.reshape(raw.shape[:-1] + (raw.shape[-1] // head_dim, head_dim))
    return rotate(normed(shaped, gain), cosine, sine)

def attend_row(record):
    queries, key_rows, value_row_block, length = record
    slot_count, kv_heads, head_dim = key_rows.shape
    grouped = queries.reshape(slot_count, kv_heads, -1, head_dim)
    scores = jnp.einsum('qkgd,tkd->kgqt', grouped, key_rows, precision=highest) * head_dim ** (-0.5)
    scores = low_back(scores)
    position = jnp.arange(slot_count)
    allowed = (position[None, :] <= position[:, None]) & (position[None, :] < length)
    scores = jnp.where(allowed, scores, -1e+30)
    row_max = lax.optimization_barrier(jnp.max(scores, axis=-1, keepdims=True))
    exp_terms = jnp.exp(scores - row_max)
    probabilities = exp_terms / lax.optimization_barrier(jnp.sum(exp_terms, axis=-1, keepdims=True))
    attended = jnp.einsum('kgqt,tkd->qkgd', low(probabilities), value_row_block, precision=highest)
    return attended.reshape(slot_count, -1)

def forward_group(hidden, lengths, adapter_ids, weights, adapters):
    attn_norm, q_norm, k_norm, ffn_norm, w_q, key_weight, value_weight, w_o, w_gate, w_up, w_down = weights
    a_q, b_q, a_k, key_second_factor, a_v, value_second_factor, a_o, b_o, a_gate, b_gate, a_up, b_up, a_down, b_down = adapters

    def pick(table):
        return jnp.take(table, adapter_ids, axis=0)

    def pick_mid(table):
        return jnp.take(table, adapter_ids, axis=1)

    def lower(rows_in, table):
        return low_back(low(jnp.einsum('gsd,gdk->gsk', rows_in, pick(table), precision=highest)))

    def project(rows_in, weight, low_rank, table):
        main_part = jnp.einsum('gsd,do->gso', rows_in, weight, precision=highest)
        return main_part + jnp.einsum('gsk,gko->gso', low_rank, pick(table), precision=highest)
    xn = low(normed(hidden, attn_norm))
    h_q = lower(xn, a_q)
    h_k = lower(xn, a_k)
    h_v = lower(xn, a_v)
    q_raw = low_back(project(xn, w_q, h_q, b_q))
    k_raw = low_back(project(xn, key_weight, h_k, key_second_factor))
    value_full = low(low_back(project(xn, value_weight, h_v, value_second_factor)))
    cosine, sine = rope_tables(ROW_SLOTS, HEAD_SIZE)
    q_rot = low(head_prep(q_raw, q_norm, cosine, sine))
    k_rot = low(head_prep(k_raw, k_norm, cosine, sine))
    value_row_block = value_full.reshape(value_full.shape[0], ROW_SLOTS, KEY_VALUE_HEADS, HEAD_SIZE)
    attended = lax.map(jax.checkpoint(attend_row), (q_rot, k_rot, value_row_block, lengths))
    attn_cat = low_back(low(attended))
    h_o = low_back(jnp.einsum('gso,gok->gsk', attn_cat, pick(a_o), precision=highest))
    attn_main = jnp.einsum('gso,od->gsd', attn_cat, w_o, precision=highest)
    attn_out = low_back(attn_main + jnp.einsum('gsk,gkd->gsd', h_o, pick(b_o), precision=highest))
    residual = hidden + attn_out
    x_two = low(normed(residual, ffn_norm))
    h_gate = lower(x_two, a_gate)
    h_up = lower(x_two, a_up)
    gate_main = jnp.einsum('gsd,fd->gsf', x_two, w_gate, precision=highest)
    gate_pre = low_back(gate_main + jnp.einsum('gsk,fgk->gsf', h_gate, pick_mid(b_gate), precision=highest))
    up_main = jnp.einsum('gsd,fd->gsf', x_two, w_up, precision=highest)
    up_pre = low_back(up_main + jnp.einsum('gsk,fgk->gsf', h_up, pick_mid(b_up), precision=highest))
    hidden_act = low(jax.nn.silu(gate_pre) * up_pre)
    h_down = low_back(jnp.einsum('gsf,fgk->gsk', hidden_act, pick_mid(a_down), precision=highest))
    ffn_main = jnp.einsum('gsf,fd->gsd', hidden_act, w_down, precision=highest)
    ffn_out = low_back(ffn_main + jnp.einsum('gsk,gkd->gsd', h_down, pick(b_down), precision=highest))
    valid = (jnp.arange(ROW_SLOTS)[None, :] < lengths[:, None]).astype(hidden.dtype)
    return (residual + ffn_out) * valid[..., None]

def widen(array):
    return array.astype(jnp.float32)

def reference(hidden_in, cotangent, lengths, adapter_ids, attn_norm, q_norm, k_norm, ffn_norm, w_q, key_weight, value_weight, w_o, w_gate, w_up, w_down, a_q, b_q, a_k, key_second_factor, a_v, value_second_factor, a_o, b_o, a_gate, b_gate, a_up, b_up, a_down, b_down):
    weights = tuple((widen(item) for item in (attn_norm, q_norm, k_norm, ffn_norm, w_q, key_weight, value_weight, w_o, w_gate, w_up, w_down)))
    adapters = tuple((widen(item) for item in (a_q, b_q, a_k, key_second_factor, a_v, value_second_factor, a_o, b_o, a_gate, b_gate, a_up, b_up, a_down, b_down)))
    groups = ROWS // ROWS_DEV
    hidden_groups = widen(hidden_in).reshape(groups, ROWS_DEV, ROW_SLOTS, MODEL_WIDTH)
    cot_groups = widen(cotangent).reshape(groups, ROWS_DEV, ROW_SLOTS, MODEL_WIDTH)
    length_groups = lengths.reshape(groups, ROWS_DEV)
    id_groups = adapter_ids.reshape(groups, ROWS_DEV)

    def step(totals, record):
        hidden, cot, length_group, id_group = record
        result, pull = jax.vjp(lambda rows_in, adapt: forward_group(rows_in, length_group, id_group, weights, adapt), hidden, adapters)
        d_hidden, d_adapters = pull(cot)
        return (tuple((total + grad for total, grad in zip(totals, d_adapters))), (result, d_hidden))
    zeros = tuple((jnp.zeros_like(item) for item in adapters))
    totals, (results, d_hiddens) = lax.scan(step, zeros, (hidden_groups, cot_groups, length_groups, id_groups))
    output = results.reshape(ROWS, ROW_SLOTS, MODEL_WIDTH).astype(jnp.bfloat16)
    d_input = d_hiddens.reshape(ROWS, ROW_SLOTS, MODEL_WIDTH).astype(jnp.bfloat16)
    return (output, d_input, totals[0], totals[1], totals[2], totals[3], totals[4], totals[5], totals[6], totals[7], totals[8], totals[9], totals[10], totals[11], totals[12], totals[13])
```

```python
import functools

import jax
import jax.numpy as jnp
from jax import lax
from jax.experimental import pallas as pl
from jax.experimental.pallas import tpu as pltpu
from jax.sharding import PartitionSpec as P

epsilon = 1e-06
rope_base = 1000000.0
low = jnp.bfloat16
full = jnp.float32
log2e = 1.4426950408889634
ffn_chunks = 3


def dot_nn(a, b):
    return lax.dot_general(a, b, (((1,), (0,)), ((), ())), preferred_element_type=full)


def dot_nt(a, b):
    return lax.dot_general(a, b, (((1,), (1,)), ((), ())), preferred_element_type=full)


def dot_tn(a, b):
    return lax.dot_general(a, b, (((0,), (0,)), ((), ())), preferred_element_type=full)


def norm_back(values, gain, grad):
    scale = lax.rsqrt(jnp.mean(values * values, axis=-1, keepdims=True) + epsilon)
    weighted = grad * gain
    inner = jnp.mean(values * weighted, axis=-1, keepdims=True)
    return scale * weighted - values * (scale * scale * scale * inner)


def normed(values, gain):
    return values * lax.rsqrt(jnp.mean(values * values, axis=-1, keepdims=True) + epsilon) * gain


def rope_tables(slot_count, head_dim):
    position = jnp.arange(slot_count).astype(full)
    exponent = jnp.arange(head_dim // 2).astype(full) * (2.0 / head_dim)
    angles = position[:, None] * (rope_base ** (-exponent))[None, :]
    cosine = jnp.cos(angles)
    sine = jnp.sin(angles)
    return (jnp.concatenate([cosine, cosine], -1), jnp.concatenate([-sine, sine], -1))


def project_kernel(x_ref, h_ref, w_ref, out_ref, *, half, low_half, group, head_dim):
    width = x_ref.shape[1]
    total = dot_nn(x_ref[:, :half], w_ref[0, 0, :half, :])
    total = total + dot_nn(x_ref[:, half:], w_ref[0, 1, :half, :])
    low_rank = 2 * low_half
    table = jnp.concatenate([w_ref[0, 0, half:, :], w_ref[0, 1, half:, :]], axis=0)
    q_width = group * head_dim
    bounds = ((0, q_width), (q_width, q_width + head_dim), (q_width + head_dim, q_width + 2 * head_dim))
    for kind, (start, stop) in enumerate(bounds):
        extra = dot_nn(h_ref[:, kind * low_rank : (kind + 1) * low_rank], table[:, start:stop])
        out_ref[0, :, start:stop] = (total[:, start:stop] + extra).astype(low)


def project(x, h, w_all, group, head_dim):
    tokens, width = x.shape
    tensor_size, _, rows, columns = w_all.shape
    block = (group + 2) * head_dim
    half = width // 2
    return pl.pallas_call(
        functools.partial(
            project_kernel, half=half, low_half=rows - half, group=group, head_dim=head_dim
        ),
        grid=(tensor_size, columns // block),
        in_specs=[
            pl.BlockSpec((tokens, width), lambda t, j: (0, 0)),
            pl.BlockSpec(h.shape, lambda t, j: (0, 0)),
            pl.BlockSpec((1, 2, rows, block), lambda t, j: (t, 0, 0, j)),
        ],
        out_specs=pl.BlockSpec((1, tokens, block), lambda t, j: (t, 0, j)),
        out_shape=jax.ShapeDtypeStruct((tensor_size, tokens, columns), low),
        name="project",
    )(x, h, w_all)


def project_back_kernel(
    d_ref, w_ref, ht_ref, dx_ref, dh_ref, gb_ref, *, half, low_half, group, head_dim
):
    step = pl.program_id(0) * pl.num_programs(1) + pl.program_id(1)

    @pl.when(step == 0)
    def _():
        dx_ref[...] = jnp.zeros_like(dx_ref)
        dh_ref[...] = jnp.zeros_like(dh_ref)

    grad = d_ref[0]
    dx_ref[:, :half] += dot_nt(grad, w_ref[0, 0, :half, :])
    dx_ref[:, half:] += dot_nt(grad, w_ref[0, 1, :half, :])
    low_rank = 2 * low_half
    table = jnp.concatenate([w_ref[0, 0, half:, :], w_ref[0, 1, half:, :]], axis=0)
    q_width = group * head_dim
    bounds = ((0, q_width), (q_width, q_width + head_dim), (q_width + head_dim, q_width + 2 * head_dim))
    for kind, (start, stop) in enumerate(bounds):
        columns = slice(kind * low_rank, (kind + 1) * low_rank)
        dh_ref[:, columns] += dot_nt(grad[:, start:stop], table[:, start:stop])
        gb_ref[0, :, start:stop] = dot_nn(ht_ref[columns, :], grad[:, start:stop]).astype(low)


def project_back(d_qkv, w_all, h_t, group, head_dim):
    tensor_size, tokens, columns = d_qkv.shape
    rows = w_all.shape[2]
    block = (group + 2) * head_dim
    low_all = h_t.shape[0]
    low_rank = low_all // 3
    half = rows - low_rank // 2
    return pl.pallas_call(
        functools.partial(
            project_back_kernel, half=half, low_half=rows - half, group=group, head_dim=head_dim
        ),
        grid=(tensor_size, columns // block),
        in_specs=[
            pl.BlockSpec((1, tokens, block), lambda t, j: (t, 0, j)),
            pl.BlockSpec((1, 2, rows, block), lambda t, j: (t, 0, 0, j)),
            pl.BlockSpec(h_t.shape, lambda t, j: (0, 0)),
        ],
        out_specs=[
            pl.BlockSpec((tokens, 2 * half), lambda t, j: (0, 0)),
            pl.BlockSpec((tokens, low_all), lambda t, j: (0, 0)),
            pl.BlockSpec((1, low_rank, block), lambda t, j: (t, 0, j)),
        ],
        out_shape=[
            jax.ShapeDtypeStruct((tokens, 2 * half), full),
            jax.ShapeDtypeStruct((tokens, low_all), full),
            jax.ShapeDtypeStruct((tensor_size, low_rank, columns), low),
        ],
        name="project_back",
    )(d_qkv, w_all, h_t)


def turned_head(raw, gain, cosine, sine):
    value = normed(raw, gain)
    return value * cosine + pltpu.roll(value, value.shape[-1] // 2, 1) * sine


def turned_head_back(raw, gain, cosine, sine, grad):
    grad = grad * cosine + pltpu.roll(grad * sine, grad.shape[-1] // 2, 1)
    return norm_back(raw, gain, grad)


def attend_kernel(
    len_ref, qkv_ref, qg_ref, kg_ref, cos_ref, sin_ref, out_ref, q_s, k_s, *, group, q_block
):
    shards, _, shard_len, _ = qkv_ref.shape
    slots = shards * shard_len
    head_dim = qg_ref.shape[1]
    scale = head_dim ** (-0.5) * log2e
    cosine = cos_ref[...]
    sine = sin_ref[...]

    def part(index):
        return qkv_ref[:, 0, :, index * head_dim : (index + 1) * head_dim].reshape(slots, head_dim)

    for g in range(group):
        q_s[g] = turned_head(part(g).astype(full), qg_ref[...], cosine, sine).astype(low)
    k_s[...] = turned_head(part(group).astype(full), kg_ref[...], cosine, sine).astype(low)
    value = part(group + 1)
    length = len_ref[pl.program_id(0)]
    per_shard = shard_len // q_block if shard_len >= q_block else 1
    shard_step = 1 if shard_len >= q_block else q_block // shard_len
    for b in range(slots // q_block):
        stop = (b + 1) * q_block
        if shard_len >= q_block:
            rows = (slice(b // per_shard, b // per_shard + 1),)
            inner = slice((b % per_shard) * q_block, (b % per_shard + 1) * q_block)
        else:
            rows = (slice(b * shard_step, (b + 1) * shard_step),)
            inner = slice(0, shard_len)

        def write(columns, block):
            out_ref[rows[0], 0, inner, columns] = block.reshape(
                rows[0].stop - rows[0].start, inner.stop - inner.start, head_dim
            )

        @pl.when(b * q_block < length)
        def _():
            keep = lax.broadcasted_iota(jnp.int32, (q_block, q_block), 1) <= lax.broadcasted_iota(
                jnp.int32, (q_block, q_block), 0
            )
            for g in range(group):
                scores = dot_nt(q_s[g, b * q_block : stop, :], k_s[:stop, :])
                terms = jnp.exp2(scores * scale)
                diagonal = jnp.where(keep, terms[:, b * q_block :], 0.0)
                if b:
                    terms = jnp.concatenate([terms[:, : b * q_block], diagonal], axis=1)
                else:
                    terms = diagonal
                total = jnp.sum(terms, axis=1, keepdims=True)
                mixed = dot_nn(terms.astype(low), value[:stop, :]) / total
                write(slice(g * head_dim, (g + 1) * head_dim), mixed.astype(low))

        @pl.when(b * q_block >= length)
        def _():
            for g in range(group):
                write(
                    slice(g * head_dim, (g + 1) * head_dim), jnp.zeros((q_block, head_dim), low)
                )


def attend(qkv, lengths, q_gain, k_gain, cosine, sine, group):
    shards, rows, shard_len, columns = qkv.shape
    head_dim = q_gain.shape[1]
    block = (group + 2) * head_dim
    heads = columns // block
    slots = shards * shard_len
    q_block = min(256, slots)
    table = pl.BlockSpec((slots, head_dim), lambda r, h, lens: (0, 0))
    gain = pl.BlockSpec((1, head_dim), lambda r, h, lens: (0, 0))
    return pl.pallas_call(
        functools.partial(attend_kernel, group=group, q_block=q_block),
        grid_spec=pltpu.PrefetchScalarGridSpec(
            num_scalar_prefetch=1,
            grid=(rows, heads),
            in_specs=[
                pl.BlockSpec((shards, 1, shard_len, block), lambda r, h, lens: (0, r, 0, h)),
                gain,
                gain,
                table,
                table,
            ],
            out_specs=pl.BlockSpec(
                (shards, 1, shard_len, group * head_dim), lambda r, h, lens: (0, r, 0, h)
            ),
            scratch_shapes=[
                pltpu.VMEM((group, slots, head_dim), low),
                pltpu.VMEM((slots, head_dim), low),
            ],
        ),
        out_shape=jax.ShapeDtypeStruct((shards, rows, shard_len, heads * group * head_dim), low),
        name="attend",
    )(lengths, qkv, q_gain, k_gain, cosine, sine)


def attend_back_kernel(
    len_ref,
    qkv_ref,
    do_ref,
    qg_ref,
    kg_ref,
    cos_ref,
    sin_ref,
    out_ref,
    q_s,
    k_s,
    kt_s,
    dq_s,
    dk_s,
    dv_s,
    *,
    group,
    q_block,
):
    shards, _, shard_len, _ = qkv_ref.shape
    slots = shards * shard_len
    head_dim = qg_ref.shape[1]
    scale = head_dim ** (-0.5)

    def part(ref, index):
        return ref[:, 0, :, index * head_dim : (index + 1) * head_dim].reshape(slots, head_dim)

    def put(index, block):
        out_ref[:, 0, :, index * head_dim : (index + 1) * head_dim] = block.astype(low).reshape(
            shards, shard_len, head_dim
        )

    for g in range(group):
        q_s[g] = turned_head(
            part(qkv_ref, g).astype(full), qg_ref[...], cos_ref[...], sin_ref[...]
        ).astype(low)
    k_rot = turned_head(
        part(qkv_ref, group).astype(full), kg_ref[...], cos_ref[...], sin_ref[...]
    )
    k_s[...] = k_rot.astype(low)
    kt_s[...] = k_rot.T.astype(low)
    dk_s[...] = jnp.zeros_like(dk_s)
    dv_s[...] = jnp.zeros_like(dv_s)
    value = part(qkv_ref, group + 1)
    length = len_ref[pl.program_id(0)]
    for b in range(slots // q_block):
        start = b * q_block
        stop = start + q_block

        @pl.when(start < length)
        def _():
            keep = lax.broadcasted_iota(jnp.int32, (q_block, q_block), 0) <= lax.broadcasted_iota(
                jnp.int32, (q_block, q_block), 1
            )
            for g in range(group):
                q_rows = q_s[g, start:stop, :]
                d_rows = part(do_ref, g)[start:stop, :]
                scores = dot_nt(k_s[:stop, :], q_rows)
                terms = jnp.exp2(scores * (scale * log2e))
                diagonal = jnp.where(keep, terms[start:, :], 0.0)
                if b:
                    terms = jnp.concatenate([terms[:start, :], diagonal], axis=0)
                else:
                    terms = diagonal
                p = terms * (1.0 / jnp.sum(terms, axis=0, keepdims=True))
                dp = dot_nt(value[:stop, :], d_rows)
                inner = jnp.sum(p * dp, axis=0, keepdims=True)
                ds = (p * (dp - inner)).astype(low)
                dq_s[g, start:stop, :] = dot_nn(kt_s[:, :stop], ds).T * scale
                dk_s[:stop, :] += dot_nn(ds, q_rows)
                dv_s[:stop, :] += dot_nn(p.astype(low), d_rows)

        @pl.when(start >= length)
        def _():
            for g in range(group):
                dq_s[g, start:stop, :] = jnp.zeros((q_block, head_dim), full)

    for g in range(group):
        put(
            g,
            turned_head_back(
                part(qkv_ref, g).astype(full), qg_ref[...], cos_ref[...], sin_ref[...], dq_s[g]
            ),
        )
    put(
        group,
        turned_head_back(
            part(qkv_ref, group).astype(full),
            kg_ref[...],
            cos_ref[...],
            sin_ref[...],
            dk_s[...] * scale,
        ),
    )
    put(group + 1, dv_s[...])


def attend_back(qkv, d_attended, lengths, q_gain, k_gain, cosine, sine, group):
    shards, rows, shard_len, columns = qkv.shape
    head_dim = q_gain.shape[1]
    block = (group + 2) * head_dim
    heads = columns // block
    slots = shards * shard_len
    q_block = min(256, slots)
    table = pl.BlockSpec((slots, head_dim), lambda r, h, lens: (0, 0))
    gain = pl.BlockSpec((1, head_dim), lambda r, h, lens: (0, 0))
    wide = pl.BlockSpec((shards, 1, shard_len, block), lambda r, h, lens: (0, r, 0, h))
    return pl.pallas_call(
        functools.partial(attend_back_kernel, group=group, q_block=q_block),
        grid_spec=pltpu.PrefetchScalarGridSpec(
            num_scalar_prefetch=1,
            grid=(rows, heads),
            in_specs=[
                wide,
                pl.BlockSpec(
                    (shards, 1, shard_len, group * head_dim), lambda r, h, lens: (0, r, 0, h)
                ),
                gain,
                gain,
                table,
                table,
            ],
            out_specs=wide,
            scratch_shapes=[
                pltpu.VMEM((group, slots, head_dim), low),
                pltpu.VMEM((slots, head_dim), low),
                pltpu.VMEM((head_dim, slots), low),
                pltpu.VMEM((group, slots, head_dim), full),
                pltpu.VMEM((slots, head_dim), full),
                pltpu.VMEM((slots, head_dim), full),
            ],
        ),
        out_shape=jax.ShapeDtypeStruct(qkv.shape, low),
        name="attend_back",
    )(lengths, qkv, d_attended, q_gain, k_gain, cosine, sine)


def ffn_kernel(
    x_ref,
    dy_ref,
    hg_ref,
    hu_ref,
    dh_ref,
    hgt_ref,
    hut_ref,
    dht_ref,
    w_ref,
    y_ref,
    dx_ref,
    yl_ref,
    dgl_ref,
    dul_ref,
    gb_ref,
    act_s,
    dgate_s,
    dup_s,
    *,
    token_block,
):
    tokens, width = x_ref.shape

    @pl.when(pl.program_id(0) == 0)
    def _():
        y_ref[...] = jnp.zeros_like(y_ref)
        dx_ref[...] = jnp.zeros_like(dx_ref)
        yl_ref[...] = jnp.zeros_like(yl_ref)
        dgl_ref[...] = jnp.zeros_like(dgl_ref)
        dul_ref[...] = jnp.zeros_like(dul_ref)

    def block(i, carry):
        rows = pl.ds(pl.multiple_of(i * token_block, token_block), token_block)
        x = x_ref[rows, :]
        dy = dy_ref[rows, :]
        gate = dot_nt(x, w_ref[0, 0, :, :width]) + dot_nt(hg_ref[rows, :], w_ref[0, 0, :, width:])
        up = dot_nt(x, w_ref[0, 1, :, :width]) + dot_nt(hu_ref[rows, :], w_ref[0, 1, :, width:])
        dact = dot_nt(dy, w_ref[0, 2, :, :width]) + dot_nt(dh_ref[rows, :], w_ref[0, 2, :, width:])
        sig = 1.0 / (1.0 + jnp.exp(-gate))
        silu = gate * sig
        act = (silu * up).astype(low)
        dgate = (dact * up * (sig * (1.0 + gate * (1.0 - sig)))).astype(low)
        dup = (dact * silu).astype(low)
        act_s[rows, :] = act
        dgate_s[rows, :] = dgate
        dup_s[rows, :] = dup
        y_ref[rows, :] += dot_nn(act, w_ref[0, 2, :, :width])
        yl_ref[rows, :] += dot_nn(act, w_ref[0, 2, :, width:])
        dx_ref[rows, :] += dot_nn(dgate, w_ref[0, 0, :, :width]) + dot_nn(
            dup, w_ref[0, 1, :, :width]
        )
        dgl_ref[rows, :] += dot_nn(dgate, w_ref[0, 0, :, width:])
        dul_ref[rows, :] += dot_nn(dup, w_ref[0, 1, :, width:])
        return carry

    lax.fori_loop(0, tokens // token_block, block, 0)
    gb_ref[0, 0] = dot_nn(hgt_ref[...], dgate_s[...]).astype(low)
    gb_ref[0, 1] = dot_nn(hut_ref[...], dup_s[...]).astype(low)
    gb_ref[0, 2] = dot_nn(dht_ref[...], act_s[...]).astype(low)


def ffn(x, dy, h_gate, h_up, dh_down, weights):
    tokens, width = x.shape
    blocks, kinds, units, augmented = weights.shape
    low_all = augmented - width
    token_block = min(512, tokens)

    def whole(array):
        return pl.BlockSpec(array.shape, lambda b: (0, 0), pipeline_mode=pl.Buffered(1))

    def kept(shape):
        return pl.BlockSpec(shape, lambda b: (0, 0), pipeline_mode=pl.Buffered(1))

    wide = (tokens, width)
    thin = (tokens, low_all)
    inputs = (x, dy, h_gate, h_up, dh_down, h_gate.T, h_up.T, dh_down.T)
    return pl.pallas_call(
        functools.partial(ffn_kernel, token_block=token_block),
        grid=(blocks,),
        in_specs=[whole(item) for item in inputs]
        + [pl.BlockSpec((1, kinds, units, augmented), lambda b: (b, 0, 0, 0))],
        out_specs=[
            kept(wide),
            kept(wide),
            kept(thin),
            kept(thin),
            kept(thin),
            pl.BlockSpec((1, kinds, low_all, units), lambda b: (b, 0, 0, 0)),
        ],
        out_shape=[
            jax.ShapeDtypeStruct(wide, full),
            jax.ShapeDtypeStruct(wide, full),
            jax.ShapeDtypeStruct(thin, full),
            jax.ShapeDtypeStruct(thin, full),
            jax.ShapeDtypeStruct(thin, full),
            jax.ShapeDtypeStruct((blocks, kinds, low_all, units), low),
        ],
        scratch_shapes=[pltpu.VMEM((tokens, units), low) for _ in range(3)],
        name="ffn",
    )(*inputs, weights)


def local(
    hidden_in,
    cotangent,
    lengths,
    adapter_ids,
    attn_norm,
    q_norm,
    k_norm,
    ffn_norm,
    w_q,
    key_weight,
    value_weight,
    w_o,
    w_gate,
    w_up,
    w_down,
    a_q,
    b_q,
    a_k,
    key_second_factor,
    a_v,
    value_second_factor,
    a_o,
    b_o,
    a_gate,
    b_gate,
    a_up,
    b_up,
    a_down,
    b_down,
):
    row_count, shard_len, width = hidden_in.shape
    tensor_size = lax.axis_size("tensor")
    dp_size = lax.axis_size("dp")
    head_dim = q_norm.shape[0]
    adapter_count, _, rank = a_q.shape
    low_all = adapter_count * rank
    tokens = row_count * shard_len
    kv_heads = key_weight.shape[1] // head_dim
    group = w_q.shape[1] // key_weight.shape[1]
    units = w_gate.shape[0]
    core = lax.axis_index("dp") % 2
    offset = lax.axis_index("tensor") * shard_len
    pair_groups = [
        [d * tensor_size + t for t in range(tensor_size) for d in (2 * p, 2 * p + 1)]
        for p in range(dp_size // 2)
    ]

    def gather(half):
        return lax.all_gather(
            half, ("dp", "tensor"), axis=0, axis_index_groups=pair_groups
        ).reshape((tensor_size, 2) + half.shape)

    def my_half(array, axis):
        size = array.shape[axis] // 2
        return lax.dynamic_slice_in_dim(array, core * size, size, axis)

    def by_head(q_part, k_part, v_part):
        pieces = []
        for h in range(kv_heads):
            pieces.append(q_part[:, h * group * head_dim : (h + 1) * group * head_dim])
            pieces.append(k_part[:, h * head_dim : (h + 1) * head_dim])
            pieces.append(v_part[:, h * head_dim : (h + 1) * head_dim])
        return jnp.concatenate(pieces, axis=1)

    def flat_a(table):
        return table.transpose(0, 2, 1).reshape(low_all, table.shape[1])

    def flat_b(table):
        return table.reshape(low_all, table.shape[2])

    def flat_mid(table):
        return table.transpose(1, 2, 0).reshape(low_all, table.shape[0])

    def unflat_a(grad):
        return grad.reshape(adapter_count, rank, -1).transpose(0, 2, 1)

    def unflat_b(grad):
        return grad.reshape(adapter_count, rank, -1)

    def unflat_mid(grad):
        return grad.reshape(adapter_count, rank, -1).transpose(2, 0, 1)

    qkv_local = by_head(w_q, key_weight, value_weight)
    qkv_low = by_head(flat_b(b_q), flat_b(key_second_factor), flat_b(value_second_factor))
    qkv_all = gather(jnp.concatenate([my_half(qkv_local, 0), my_half(qkv_low, 0)], axis=0))
    out_local = jnp.concatenate([w_o, flat_a(a_o).T], axis=1)
    out_all = gather(my_half(out_local, 0)).reshape(tensor_size, -1, width + low_all)
    chunk_units = units // ffn_chunks
    ffn_all = []
    tables = (
        (w_gate, flat_mid(b_gate).T),
        (w_up, flat_mid(b_up).T),
        (w_down, flat_mid(a_down).T),
    )
    for c in range(ffn_chunks):
        halves = []
        for main, thin in tables:
            start = c * chunk_units + core * (chunk_units // 2)
            halves.append(
                jnp.concatenate(
                    [
                        lax.dynamic_slice_in_dim(main, start, chunk_units // 2, 0),
                        lax.dynamic_slice_in_dim(thin, start, chunk_units // 2, 0),
                    ],
                    axis=1,
                )
            )
        ffn_all.append(
            gather(jnp.stack(halves)).reshape(
                2 * tensor_size, 3, chunk_units // 2, width + low_all
            )
        )

    cosine, sine = rope_tables(shard_len * tensor_size, head_dim)
    attn_gain = attn_norm.astype(full)
    ffn_gain = ffn_norm.astype(full)
    q_gain = q_norm.astype(full)[None]
    k_gain = k_norm.astype(full)[None]
    slot_local = offset + jnp.arange(shard_len)
    valid = (slot_local[None, :] < lengths[:, None]).astype(full).reshape(tokens, 1)
    mine = jnp.arange(low_all)[None, :] // rank == adapter_ids[:, None]
    mask = jnp.broadcast_to(mine[:, None, :], (row_count, shard_len, low_all)).reshape(
        tokens, low_all
    )

    def masked(values):
        repeated = jnp.concatenate([mask] * (values.shape[1] // low_all), axis=1)
        return jnp.where(repeated, values, 0.0)

    hidden32 = hidden_in.reshape(tokens, width).astype(full)
    d_out = cotangent.reshape(tokens, width).astype(full) * valid
    d_ffn = d_out.astype(low)
    b_down_flat = flat_b(b_down)
    b_o_flat = flat_b(b_o)
    dh_down = masked(dot_nt(d_ffn, b_down_flat)).astype(low)

    xn = normed(hidden32, attn_gain).astype(low)
    a_qkv = jnp.concatenate([flat_a(a_q), flat_a(a_k), flat_a(a_v)], axis=0)
    a_gu = jnp.concatenate([flat_a(a_gate), flat_a(a_up)], axis=0)
    h_qkv = masked(dot_nt(xn, a_qkv)).astype(low)
    sent = project(xn, h_qkv, qkv_all, group, head_dim)
    qkv = lax.all_to_all(sent, "tensor", 0, 0).reshape(
        tensor_size, row_count, shard_len, sent.shape[2]
    )
    attended = attend(qkv, lengths, q_gain, k_gain, cosine, sine, group)
    attn_cat = lax.all_to_all(attended.reshape(tensor_size, tokens, -1), "tensor", 0, 0)
    out_sum = jnp.einsum("tso,tod->sd", attn_cat, out_all, preferred_element_type=full)
    h_o = masked(out_sum[:, width:]).astype(low)
    residual = hidden32 + out_sum[:, :width] + dot_nn(h_o, b_o_flat)
    x2 = normed(residual, ffn_gain).astype(low)
    h_gu = masked(dot_nt(x2, a_gu)).astype(low)
    results = [
        ffn(x2, d_ffn, h_gu[:, :low_all], h_gu[:, low_all:], dh_down, item) for item in ffn_all
    ]
    ffn_sum, d_x2, h_down, dh_gate, dh_up = (
        functools.reduce(lambda a, b: a + b, [item[i] for item in results]) for i in range(5)
    )
    h_down = masked(h_down).astype(low)
    output = ((residual + ffn_sum + dot_nn(h_down, b_down_flat)) * valid).astype(low)
    dh_gu = masked(jnp.concatenate([dh_gate, dh_up], axis=1)).astype(low)
    d_x2 = d_x2 + dot_nn(dh_gu, a_gu)
    d_residual = d_out + norm_back(residual, ffn_gain, d_x2)
    d_attn = d_residual.astype(low)
    dh_o = masked(dot_nt(d_attn, b_o_flat)).astype(low)
    d_cat = jnp.einsum(
        "sd,tod->tso",
        jnp.concatenate([d_attn, dh_o], axis=1),
        out_all,
        preferred_element_type=full,
    ).astype(low)
    d_attended = lax.all_to_all(d_cat, "tensor", 0, 0).reshape(attended.shape)
    d_sent = attend_back(qkv, d_attended, lengths, q_gain, k_gain, cosine, sine, group)
    d_qkv = lax.all_to_all(d_sent.reshape(sent.shape), "tensor", 0, 0)
    d_xn, dh_qkv, grad_b_qkv = project_back(d_qkv, qkv_all, h_qkv.T, group, head_dim)
    dh_qkv = masked(dh_qkv).astype(low)
    d_xn = d_xn + dot_nn(dh_qkv, a_qkv)
    d_input = (d_residual + norm_back(hidden32, attn_gain, d_xn)).astype(low)

    grad_b_down = dot_tn(h_down, d_ffn).astype(low)
    grad_a_gu = dot_tn(dh_gu, x2).astype(low)
    grad_b_o = dot_tn(h_o, d_attn).astype(low)
    grad_a_o = jnp.einsum("sk,tso->tko", dh_o, attn_cat, preferred_element_type=full).astype(low)
    grad_ffn = jnp.stack([item[5] for item in results])
    grad_ffn = grad_ffn.reshape(ffn_chunks, tensor_size, 2, 3, low_all, chunk_units // 2)
    grad_ffn = grad_ffn.transpose(1, 3, 4, 0, 2, 5).reshape(tensor_size, 3 * low_all, units)
    grad_a_qkv = dot_tn(dh_qkv, xn).astype(low)

    def reduce_all(split, whole):
        lengths_split = [item.shape[1] * item.shape[2] for item in split]
        parts = [item.reshape(tensor_size, -1, 128) for item in split]
        joined = jnp.concatenate(whole, axis=0)
        parts.append(joined.reshape(tensor_size, -1, 128))
        sums = lax.psum_scatter(jnp.concatenate(parts, axis=1), "tensor", scatter_dimension=0)
        sums = lax.psum(sums, "dp")
        outs = []
        start = 0
        for item, count in zip(split, lengths_split):
            outs.append(sums[start : start + count // 128].reshape(item.shape[1:]).astype(full))
            start += count // 128
        total = lax.all_gather(sums[start:], "tensor", axis=0).reshape(joined.shape).astype(full)
        return outs, total

    (grad_ffn, grad_a_o), early = reduce_all(
        (grad_ffn, grad_a_o), (grad_b_down, grad_a_gu, grad_b_o)
    )
    (grad_b_qkv,), late = reduce_all((grad_b_qkv,), (grad_a_qkv,))

    def of_kind(array, start, size):
        step = (group + 2) * head_dim
        return jnp.concatenate(
            [array[:, h * step + start : h * step + start + size] for h in range(kv_heads)], axis=1
        )

    def piece(array, index):
        return array[index * low_all : (index + 1) * low_all]

    return (
        output.reshape(hidden_in.shape),
        d_input.reshape(hidden_in.shape),
        unflat_a(piece(late, 0)),
        unflat_b(of_kind(grad_b_qkv, 0, group * head_dim)),
        unflat_a(piece(late, 1)),
        unflat_b(of_kind(grad_b_qkv, group * head_dim, head_dim)),
        unflat_a(piece(late, 2)),
        unflat_b(of_kind(grad_b_qkv, (group + 1) * head_dim, head_dim)),
        unflat_a(grad_a_o),
        unflat_b(piece(early, 3)),
        unflat_a(piece(early, 1)),
        unflat_mid(piece(grad_ffn, 0)),
        unflat_a(piece(early, 2)),
        unflat_mid(piece(grad_ffn, 1)),
        unflat_mid(piece(grad_ffn, 2)),
        unflat_b(piece(early, 0)),
    )


def solution(mesh):
    placed = (
        P("dp", "tensor", None),
        P("dp", "tensor", None),
        P("dp"),
        P("dp"),
        P(),
        P(),
        P(),
        P(),
        P(None, "tensor"),
        P(None, "tensor"),
        P(None, "tensor"),
        P("tensor", None),
        P("tensor", None),
        P("tensor", None),
        P("tensor", None),
        P(),
        P(None, None, "tensor"),
        P(),
        P(None, None, "tensor"),
        P(),
        P(None, None, "tensor"),
        P(None, "tensor", None),
        P(),
        P(),
        P("tensor", None, None),
        P(),
        P("tensor", None, None),
        P("tensor", None, None),
        P(),
    )
    return jax.shard_map(
        local,
        mesh=mesh,
        in_specs=placed,
        out_specs=(
            P("dp", "tensor", None),
            P("dp", "tensor", None),
            P(),
            P(None, None, "tensor"),
            P(),
            P(None, None, "tensor"),
            P(),
            P(None, None, "tensor"),
            P(None, "tensor", None),
            P(),
            P(),
            P("tensor", None, None),
            P(),
            P("tensor", None, None),
            P("tensor", None, None),
            P(),
        ),
        check_vma=False,
    )
```
